32 devices in a mesh: dp: 2 (over y), seq: 8 (over z, x), head: 2 (over core).
Axes of the slice: x: 2, y: 2, z: 4, core: 2. Of those that a mesh axis runs over, the one named last changes fastest.
Arguments:
- q_raw: bfloat16 [6144, 5120], P(('dp', 'seq'), 'head'), parts along dimension 0, may hold values from -10 to 10
- k_raw: bfloat16 [6144, 5120], P(('dp', 'seq'), 'head'), parts along dimension 0, may hold values from -10 to 10
- values: bfloat16 [6144, 5120], P(('dp', 'seq'), 'head'), parts along dimension 0, may hold values from -6 to 6
- out_grad: bfloat16 [6144, 5120], P(('dp', 'seq'), 'head'), parts along dimension 0, may hold values from -40 to 40
- q_gain: float32 [5120], P('head'), may hold values from 0.1 to 1.9
- k_gain: float32 [5120], P('head'), may hold values from 0.1 to 1.9
- clip_lengths: int32 [128], P('dp'), parts along dimension 0, may hold values from 1 to 384, 3072 in all
- clip_grid: int32 [128, 2], P('dp'), parts along dimension 0, may hold values from 2 to 16
Outputs:
- attn_out: bfloat16 [6144, 5120], P(('dp', 'seq'), 'head'), parts along dimension 0
- q_grad: bfloat16 [6144, 5120], P(('dp', 'seq'), 'head'), parts along dimension 0
- k_grad: bfloat16 [6144, 5120], P(('dp', 'seq'), 'head'), parts along dimension 0
- v_grad: bfloat16 [6144, 5120], P(('dp', 'seq'), 'head'), parts along dimension 0
- q_gain_grad: float32 [10240], P(('dp', 'head')), parts along dimension 0
- k_gain_grad: float32 [10240], P(('dp', 'head')), parts along dimension 0
The draws below stay inside these ranges and needn't reach their ends.
There are 2 independent parts, one for each index of `dp`. The reference program is written for one: setup_inputs(seed, part) draws one part's arguments, and reference() takes and returns one part's arrays. A program takes and returns all parts, laid end to end along the dimension named above; an argument that names none is the same for every part. Nothing has to cross between parts.
Inputs may be any that keep to these rules, and one draw needn't show every extreme that they name: `clip_lengths`: the clips lie end to end in this order and fill all 3072 tokens; the longest holds exactly 384. `clip_grid`: a clip's tokens run frame by frame and row by row within a frame; its last frame may be partial.
All inputs are finite; a program needn't handle non-finite values.
Results may differ from the reference program's by a relative error of at most 0.012.
Values may be sent and summed in bfloat16 or wider, within the bound.
No kernel may reach another device: no remote copies, remote signals or barrier semaphores. Data moves between devices by JAX's collectives and lax.ppermute only.
A program may use at most 192 MiB of HBM per device.

```python
import math
import jax
import jax.numpy as jnp
import numpy as np
from jax import lax

HEADS = 40
HD = 128
WIDTH = 5120
TOK_DEV = 384
CLIPS = 64
LENGTH = 3072
N_SEQ = 8


def scaled_field(key_in, trend):
    key_col, key_row, key_base = jax.random.split(key_in, 3)
    col_scale = 10.0 ** (trend + 0.5 * jax.random.uniform(key_col, (WIDTH,), jnp.float32))
    row_scale = 10.0 ** jax.random.uniform(key_row, (LENGTH, 1), jnp.float32)
    base_val = jnp.clip(jax.random.normal(key_base, (LENGTH, WIDTH), jnp.float32), -4.0, 4.0)
    return base_val * row_scale * col_scale[None, :]


def drawn_pair(key_in):
    subkeys = jax.random.split(key_in, 2)
    head_of = (jnp.arange(WIDTH) // HD).astype(jnp.float32)
    trend = 0.5 * head_of / max(HEADS - 1, 1)
    query_val = scaled_field(subkeys[0], trend)
    key_val = scaled_field(subkeys[1], trend)
    return (0.01 * query_val, 0.01 * key_val)


def draw_q_raw(key, part):
    return drawn_pair(jax.random.fold_in(key, 7))[0].astype(jnp.bfloat16)


def draw_k_raw(key, part):
    return drawn_pair(jax.random.fold_in(key, 7))[1].astype(jnp.bfloat16)


def draw_out_grad(key, part):
    key_row, key_base = jax.random.split(jax.random.fold_in(key, 13), 2)
    rise = 3.0 ** (jnp.arange(LENGTH, dtype=jnp.float32) / LENGTH)
    row_scale = 10.0 ** jax.random.uniform(key_row, (LENGTH, 1), jnp.float32)
    base_val = jnp.clip(jax.random.normal(key_base, (LENGTH, WIDTH), jnp.float32), -4.0, 4.0)
    return (0.3 * base_val * row_scale * rise[:, None]).astype(jnp.bfloat16)


def plant(result, key, smallest, top_value):
    extent = result.shape
    index_at = [jax.random.randint(jax.random.fold_in(key, axis), (), 0, extent[axis]) for axis in range(len(extent))]
    result = result.at[tuple(index_at)].set(smallest)
    longest = extent.index(max(extent))
    index_at[longest] = (index_at[longest] + 1) % extent[longest]
    return result.at[tuple(index_at)].set(top_value)


def shard_levels(key, extent, cuts, least, high):
    factor_of, own = 1.0, jax.random.fold_in(key, 6)
    for dim, blocks in cuts:
        steps = jnp.exp(jax.random.uniform(jax.random.fold_in(own, dim), (blocks,), jnp.float32, least / len(cuts), high / len(cuts)))
        factor_of = factor_of * jnp.repeat(steps, extent[dim] // blocks).reshape([-1 if axis == dim else 1 for axis in range(len(extent))])
    return factor_of


def split_up(number_of, total, reach, slope):
    weights = [(1 << 20) // math.isqrt(standing ** slope) + 1 for standing in range(2, number_of + 1)]
    rest, given = total - reach - (number_of - 1), [1] * (number_of - 1)
    while rest > 0:
        candidates = [i for i in range(number_of - 1) if given[i] < reach]
        whole, budget = sum([weights[i] for i in candidates]), rest
        for i in candidates:
            more = min(reach - given[i], max(1, budget * weights[i] // whole), rest)
            given[i] = given[i] + more
            rest = rest - more
    return np.array([reach] + given)


def ragged(stream_key, number_of, total, reach, lean):
    if number_of == 2:
        one = jax.random.randint(stream_key, (), max(1, total - reach), min(reach, total - 1) + 1)
        return jnp.stack([one, total - one])
    tallies = jnp.asarray(split_up(number_of, total, reach, lean), jnp.int32)
    twos = (number_of - 1) // 2
    donor, sink = tallies[1:1 + 2 * twos:2], tallies[2:2 + 2 * twos:2]
    slack = jnp.minimum(donor - 1, reach - sink)
    shifted = jax.random.randint(jax.random.fold_in(stream_key, 1), (twos,), 0, 1 << 20) % (slack + 1)
    tallies = tallies.at[1:1 + 2 * twos:2].set(donor - shifted).at[2:2 + 2 * twos:2].set(sink + shifted)
    return tallies[jax.random.permutation(jax.random.fold_in(stream_key, 2), number_of)]


def normal_values(stream_key, shape, width, most, pieces=(), kind=jnp.bfloat16):
    gain = shard_levels(stream_key, shape, pieces, -0.22, 0.18) if pieces else 1.0
    drawn = jax.random.normal(stream_key, shape, jnp.float32) * width * gain
    return jnp.minimum(jnp.maximum(drawn, -most), most).astype(kind)


def setup_inputs(seed: int = 0, part: int = 0) -> dict:
    keys = jax.random.split(jax.random.key(seed), 9)
    part_keys = jax.random.split(jax.random.fold_in(keys[8], part), 9)
    q_raw = draw_q_raw(jax.random.fold_in(jax.random.fold_in(keys[8], part), 71), part)
    k_raw = draw_k_raw(jax.random.fold_in(jax.random.fold_in(keys[8], part), 71), part)
    values = normal_values(part_keys[2], (LENGTH, WIDTH), 1.0, 6.0, ((0, 8), (1, 2)))
    out_grad = draw_out_grad(jax.random.fold_in(jax.random.fold_in(keys[8], part), 71), part)
    q_gain = jnp.clip(1.0 + 0.18 * jax.random.normal(keys[4], (WIDTH,), jnp.float32), 0.1, 1.9)
    k_gain = jnp.clip(1.0 + 0.18 * jax.random.normal(keys[5], (WIDTH,), jnp.float32), 0.1, 1.9)
    clip_lengths = ragged(part_keys[6], CLIPS, LENGTH, TOK_DEV, 2).astype(jnp.int32)
    clip_grid = plant(jax.random.randint(part_keys[7], (CLIPS, 2), 2, 17), jax.random.fold_in(part_keys[7], 1), 2, 16).astype(jnp.int32)
    return dict(q_raw=q_raw, k_raw=k_raw, values=values, out_grad=out_grad, q_gain=q_gain, k_gain=k_gain, clip_lengths=clip_lengths, clip_grid=clip_grid)


def rope_freqs():
    half_dim = HD // 2
    span_sizes = (half_dim - 2 * (half_dim // 3), half_dim // 3, half_dim // 3)
    tables = []
    for span_len in span_sizes:
        exponent = jnp.arange(0, 2 * span_len, 2, dtype=jnp.float32) / (2 * span_len)
        tables.append(1.0 / 10000.0 ** exponent)
    return tables

def clip_bounds(clip_lengths, positions):
    ends_at = jnp.cumsum(clip_lengths).astype(jnp.int32)
    starts_at = (ends_at - clip_lengths).astype(jnp.int32)
    member = (positions[:, None] >= starts_at[None, :]) & (positions[:, None] < ends_at[None, :])
    return (member, starts_at)

def token_labels(clip_lengths, positions):
    member, starts_at = clip_bounds(clip_lengths, positions)
    numbers = jnp.arange(CLIPS, dtype=jnp.int32)
    labels = lax.optimization_barrier(jnp.sum(jnp.where(member, numbers[None, :], 0), axis=1)).astype(jnp.int32)
    return jnp.where(jnp.any(member, axis=1), labels, -1).astype(jnp.int32)

def token_angles(clip_lengths, clip_grid, positions):
    member, starts_at = clip_bounds(clip_lengths, positions)

    def pick_value(table):
        return lax.optimization_barrier(jnp.sum(jnp.where(member, table[None, :], 0), axis=1)).astype(jnp.int32)
    first_pos = pick_value(starts_at)
    height = jnp.maximum(pick_value(clip_grid[:, 0]), 1)
    across = jnp.maximum(pick_value(clip_grid[:, 1]), 1)
    offset = positions - first_pos
    plane_size = height * across
    frame_pos = offset // plane_size
    row_pos = offset % plane_size // across
    col_pos = offset % across
    freq_t, freq_h, freq_w = rope_freqs()
    return jnp.concatenate([frame_pos.astype(jnp.float32)[:, None] * freq_t[None, :], row_pos.astype(jnp.float32)[:, None] * freq_h[None, :], col_pos.astype(jnp.float32)[:, None] * freq_w[None, :]], axis=1)

def rotate(tensor, angles, sign):
    token_count, head_count, head_dim = tensor.shape
    pair_view = tensor.reshape(token_count, head_count, head_dim // 2, 2)
    even_part = pair_view[..., 0]
    odd_part = pair_view[..., 1]
    cosine = jnp.cos(angles)[:, None, :]
    sine_val = (sign * jnp.sin(angles))[:, None, :]
    turned = jnp.stack([even_part * cosine - odd_part * sine_val, even_part * sine_val + odd_part * cosine], axis=-1)
    return turned.reshape(token_count, head_count, head_dim)

def normalize(raw_rows, gain_row):
    full_rows = raw_rows.astype(jnp.float32)
    mean_sq = lax.optimization_barrier(jnp.mean(full_rows * full_rows, axis=1, keepdims=True))
    inv_rms = lax.rsqrt(mean_sq + 1e-06)
    unit_rows = full_rows * inv_rms
    return (unit_rows, inv_rms, unit_rows * gain_row[None, :])

def reference(q_raw, k_raw, values, out_grad, q_gain, k_gain, clip_lengths, clip_grid):
    positions = jnp.arange(LENGTH, dtype=jnp.int32)
    labels = token_labels(clip_lengths, positions)
    angles = token_angles(clip_lengths, clip_grid, positions)
    q_unit, q_inv, q_pre = normalize(q_raw, q_gain)
    k_unit, k_inv, k_pre = normalize(k_raw, k_gain)
    q_rot = rotate(q_pre.reshape(LENGTH, HEADS, HD), angles, 1.0).astype(jnp.bfloat16)
    k_rot = rotate(k_pre.reshape(LENGTH, HEADS, HD), angles, 1.0).astype(jnp.bfloat16)
    value_rows = values.reshape(LENGTH, HEADS, HD)
    grad_rows = out_grad.reshape(LENGTH, HEADS, HD)
    margin = ((TOK_DEV, TOK_DEV), (0, 0), (0, 0))
    key_pad = jnp.pad(k_rot, margin)
    value_pad = jnp.pad(value_rows, margin)
    label_pad = jnp.pad(labels, (TOK_DEV, TOK_DEV), constant_values=-1)
    score_scale = 1.0 / math.sqrt(HD)

    def block_step(carried, block_index):
        key_acc, value_acc = carried
        first_row = (block_index * TOK_DEV).astype(jnp.int32)

        def take_rows(array, row_span):
            return lax.dynamic_slice_in_dim(array, first_row, row_span, 0)
        queries = take_rows(q_rot, TOK_DEV).astype(jnp.float32)
        keys_win = take_rows(key_pad, 3 * TOK_DEV).astype(jnp.float32)
        vals_win = take_rows(value_pad, 3 * TOK_DEV).astype(jnp.float32)
        grads_blk = take_rows(grad_rows, TOK_DEV).astype(jnp.float32)
        query_labels = take_rows(labels, TOK_DEV)
        window_labels = take_rows(label_pad, 3 * TOK_DEV)
        scores = jnp.einsum('qhd,khd->hqk', queries, keys_win) * score_scale
        allowed = (query_labels[:, None] == window_labels[None, :])[None]
        scores = jnp.where(allowed, scores, -jnp.inf)
        row_max = lax.optimization_barrier(jnp.max(scores, axis=2, keepdims=True))
        log_total = row_max + jnp.log(lax.optimization_barrier(jnp.sum(jnp.exp(scores - row_max), axis=2, keepdims=True)))
        weights = jnp.exp(scores - log_total)
        weights_b = lax.optimization_barrier(weights.astype(jnp.bfloat16)).astype(jnp.float32)
        attended = jnp.einsum('hqk,khd->qhd', weights_b, vals_win).astype(jnp.bfloat16)
        row_delta = lax.optimization_barrier(jnp.sum(grads_blk * attended.astype(jnp.float32), axis=2))
        prob_grad = jnp.einsum('qhd,khd->hqk', grads_blk, vals_win)
        score_grad = weights * (prob_grad - row_delta.T[:, :, None]) * score_scale
        score_b = lax.optimization_barrier(score_grad.astype(jnp.bfloat16)).astype(jnp.float32)
        query_grad = jnp.einsum('hqk,khd->qhd', score_b, keys_win)
        key_part = jnp.einsum('hqk,qhd->khd', score_b, queries)
        value_part = jnp.einsum('hqk,qhd->khd', weights_b, grads_blk)
        key_acc = lax.dynamic_update_slice_in_dim(key_acc, take_rows(key_acc, 3 * TOK_DEV) + key_part, first_row, 0)
        value_acc = lax.dynamic_update_slice_in_dim(value_acc, take_rows(value_acc, 3 * TOK_DEV) + value_part, first_row, 0)
        return ((key_acc, value_acc), (attended, query_grad))
    zero_rows = jnp.zeros((LENGTH + 2 * TOK_DEV, HEADS, HD), jnp.float32)
    (key_acc, value_acc), (attended, query_grad) = lax.scan(block_step, (zero_rows, zero_rows), jnp.arange(N_SEQ, dtype=jnp.int32))
    attn_out = attended.reshape(LENGTH, WIDTH)
    query_grad = query_grad.reshape(LENGTH, HEADS, HD)
    key_grad_rot = key_acc[TOK_DEV:TOK_DEV + LENGTH]
    v_grad = value_acc[TOK_DEV:TOK_DEV + LENGTH].reshape(LENGTH, WIDTH).astype(jnp.bfloat16)

    def unwind(rot_grad, unit_rows, inv_rms, gain_row):
        pre_grad = rotate(rot_grad, angles, -1.0).reshape(LENGTH, WIDTH)
        gain_grad = lax.optimization_barrier(jnp.sum(pre_grad * unit_rows, axis=0))
        unit_grad = pre_grad * gain_row[None, :]
        inner_mean = lax.optimization_barrier(jnp.mean(unit_grad * unit_rows, axis=1, keepdims=True))
        return ((inv_rms * (unit_grad - unit_rows * inner_mean)).astype(jnp.bfloat16), gain_grad)
    q_grad, q_gain_grad = unwind(query_grad, q_unit, q_inv, q_gain)
    k_grad, k_gain_grad = unwind(key_grad_rot, k_unit, k_inv, k_gain)
    return (attn_out, q_grad, k_grad, v_grad, q_gain_grad, k_gain_grad)
```

```python
import functools
import math

import jax
import jax.numpy as jnp
from jax import lax
from jax.experimental import pallas as pl
from jax.experimental.pallas import tpu as pltpu
from jax.sharding import PartitionSpec as P

HD = 128
TILE = 128
LAG = 2
NEG = -1e30
SCALE = 1.0 / math.sqrt(HD)
EXP2_SCALE = SCALE * math.log2(math.e)


def passed_along(value, axis, by):
    count = lax.axis_size(axis)
    pairs = [(i, i + by) for i in range(count) if 0 <= i + by < count]
    return lax.ppermute(value, axis, pairs)


def sum_over(value, axis):
    count = lax.axis_size(axis)
    if count & (count - 1):
        return lax.psum(value, axis)
    step = 1
    while step < count:
        value = value + lax.ppermute(value, axis, [(i, i ^ step) for i in range(count)])
        step *= 2
    return value


def lane_freqs():
    half_dim = HD // 2
    spans = (half_dim - 2 * (half_dim // 3), half_dim // 3, half_dim // 3)
    tables = []
    for span_len in spans:
        exponent = jnp.arange(0, 2 * span_len, 2, dtype=jnp.float32) / (2 * span_len)
        tables.append(jnp.repeat(1.0 / 10000.0**exponent, 2))
    return tables


def window_tables(clip_lengths, clip_grid, positions):
    clips = clip_lengths.shape[0]
    ends_at = jnp.cumsum(clip_lengths)
    starts_at = ends_at - clip_lengths
    member = (positions[:, None] >= starts_at[None, :]) & (positions[:, None] < ends_at[None, :])

    def pick(table):
        return jnp.sum(jnp.where(member, table[None, :], 0), axis=1)

    labels = pick(jnp.arange(1, clips + 1, dtype=jnp.int32)) - 1
    offset = positions - pick(starts_at)
    height = jnp.maximum(pick(clip_grid[:, 0]), 1)
    across = jnp.maximum(pick(clip_grid[:, 1]), 1)
    plane = height * across
    frame_pos = offset // plane
    row_pos = offset % plane // across
    col_pos = offset % across
    freq_t, freq_h, freq_w = lane_freqs()
    angles = jnp.concatenate(
        [
            frame_pos.astype(jnp.float32)[:, None] * freq_t[None, :],
            row_pos.astype(jnp.float32)[:, None] * freq_h[None, :],
            col_pos.astype(jnp.float32)[:, None] * freq_w[None, :],
        ],
        axis=1,
    )
    sign = jnp.where(jnp.arange(HD) % 2 == 0, -1.0, 1.0).astype(jnp.float32)
    return labels, jnp.cos(angles), jnp.sin(angles) * sign[None, :]


def step_kernel(rows, attn, fin, more, names_in, names_out, *refs):
    r = dict(zip(names_in + names_out, refs))
    f32, bf16 = jnp.float32, jnp.bfloat16
    first = pl.program_id(0) == 0
    even = (lax.broadcasted_iota(jnp.int32, (rows, HD), 1) & 1) == 0
    labk = r["labk"]
    own = slice(rows, 2 * rows)
    need_left = labk[own, :] == labk[rows - 1 : rows, :]
    need_right = labk[own, :] == labk[2 * rows : 2 * rows + 1, :]

    def swapped(x):
        return jnp.where(even, pltpu.roll(x, HD - 1, 1), pltpu.roll(x, 1, 1))

    def turned(x, at):
        return x * r["cos"][at, :] + swapped(x) * r["sin"][at, :]

    def turned_back(x):
        return x * r["cos"][own, :] - swapped(x) * r["sin"][own, :]

    def dot(a, b, ca, cb):
        return lax.dot_general(a, b, (((ca,), (cb,)), ((), ())), preferred_element_type=f32)

    if attn:
        ksc, vsc, ktsc, vtsc, qsc, dksc, dvsc, dqsc = refs[len(names_in) + len(names_out) :]
        sources = (
            (r["recv_l"][0], r["recv_l"][1], labk[0:rows, :] == labk[rows : rows + 1, :]),
            (r["k"][...], r["v"][...], None),
            (
                r["recv_r"][0],
                r["recv_r"][1],
                labk[2 * rows : 3 * rows, :] == labk[2 * rows - 1 : 2 * rows, :],
            ),
        )
        for seg, (k_src, v_src, valid) in enumerate(sources):
            at = slice(seg * rows, (seg + 1) * rows)
            k_seg = turned(k_src.astype(f32) * r["invk"][at, :] * r["k_gain"][...], at)
            v_seg = v_src.astype(f32)
            if valid is not None:
                k_seg = jnp.where(valid, k_seg, 0.0)
                v_seg = jnp.where(valid, v_seg, 0.0)
            ksc[at, :] = k_seg.astype(bf16)
            vsc[at, :] = v_seg.astype(bf16)
            ktsc[:, at] = k_seg.T.astype(bf16)
            vtsc[:, at] = v_seg.T.astype(bf16)
        q_unit = r["q"][...].astype(f32) * r["invq"][...]
        qsc[...] = turned(q_unit * r["q_gain"][...], own).astype(bf16)
        dksc[...] = jnp.zeros_like(dksc)
        dvsc[...] = jnp.zeros_like(dvsc)
        tiles = rows // TILE
        reach = (2 * tiles + 1) * TILE

        def tile_step(i, carry):
            at = pl.multiple_of(i * TILE, TILE)
            qs, ks = pl.ds(at, TILE), pl.ds(at, reach)
            q_tile, g_tile = qsc[qs, :], r["g"][qs, :]
            s = dot(ksc[ks, :], q_tile, 1, 1)
            allowed = labk[ks, :] == r["labq"][pl.ds(pl.multiple_of(i * 8, 8), 8), :][0:1, :]
            s = jnp.where(allowed, s, NEG)
            top = jnp.max(s, axis=0, keepdims=True)
            p = jnp.exp2((s - top) * EXP2_SCALE)
            w = p * (1.0 / jnp.sum(p, axis=0, keepdims=True))
            wb = w.astype(bf16)
            out_t = dot(vtsc[:, ks], wb, 1, 0)
            g_t = g_tile.astype(f32).T
            delta = jnp.sum(out_t.astype(bf16).astype(f32) * g_t, axis=0, keepdims=True)
            r["attn_out"][qs, :] = out_t.T.astype(bf16)
            dp = dot(vsc[ks, :], g_tile, 1, 1)
            ds = (w * (dp - delta)).astype(bf16)
            dqsc[qs, :] = dot(ktsc[:, ks], ds, 1, 0).T * SCALE
            dksc[ks, :] += dot(ds, q_tile, 1, 0)
            dvsc[ks, :] += dot(wb, g_tile, 1, 0)
            return carry

        lax.fori_loop(0, tiles, tile_step, 0)

        for part, acc, scale in ((0, dksc, SCALE), (1, dvsc, 1.0)):
            to_left = acc[0:rows, :] * scale
            to_right = acc[2 * rows : 3 * rows, :] * scale
            if more:
                ahead = r["k_next" if part == 0 else "v_next"][...].astype(f32)
                to_left = jnp.where(need_left, ahead, to_left)
                to_right = jnp.where(need_right, ahead, to_right)
            r["send_l"][part] = to_left.astype(bf16)
            r["send_r"][part] = to_right.astype(bf16)
            r["dkv"][part] = acc[own, :] * scale
        q_unit = r["q"][...].astype(f32) * r["invq"][...]
        dq_pre = turned_back(dqsc[...])
        r["gq"][...] = jnp.sum(dq_pre * q_unit, axis=0, keepdims=True)
        uq = dq_pre * r["q_gain"][...]
        r["uq"][...] = uq

        @pl.when(first)
        def _():
            r["inq"][...] = r["inq_was"][...]

        r["inq"][...] += uq * q_unit

    if fin:
        totals = []
        for part in (0, 1):
            total = r["dkv_was"][part]
            total += jnp.where(need_left, r["recv_l"][part].astype(f32), 0.0)
            total += jnp.where(need_right, r["recv_r"][part].astype(f32), 0.0)
            totals.append(total)
        r["v_grad"][...] = totals[1].astype(bf16)
        k_unit = r["k_fin"][...].astype(f32) * r["invk"][own, :]
        dk_pre = turned_back(totals[0])
        r["gk"][...] = jnp.sum(dk_pre * k_unit, axis=0, keepdims=True)
        uk = dk_pre * r["k_gain_fin"][...]
        r["uk"][...] = uk

        @pl.when(first)
        def _():
            r["ink"][...] = r["ink_was"][...]

        r["ink"][...] += uk * k_unit


def run_step(step, groups, per, rows, width, a):
    attn, fin, more = step < groups, step >= LAG, step + LAG < groups
    f32, bf16 = jnp.float32, jnp.bfloat16
    ins, outs, aliases = [], [], {}

    def columns(group, height=rows):
        return pl.BlockSpec((height, HD), lambda j: (0, group * per + j))

    def whole(array):
        return pl.BlockSpec(array.shape, lambda j: (0,) * array.ndim)

    pair = pl.BlockSpec((2, rows, HD), lambda j: (0, 0, j))
    pair_shape = (2, rows, per * HD)

    def add_in(name, array, spec):
        ins.append((name, array, spec))

    def add_out(name, shape, dtype, spec, was=None):
        if was is not None:
            aliases[len(ins)] = len(outs)
            add_in(name + "_buf", was, pl.BlockSpec(memory_space=pl.ANY))
        outs.append((name, jax.ShapeDtypeStruct(shape, dtype), spec))

    for name in ("cos", "sin", "invk", "labk"):
        add_in(name, a[name], whole(a[name]))
    add_in("recv_l", a["recv_l"][step], pair)
    add_in("recv_r", a["recv_r"][step], pair)
    if attn:
        for name in ("labq", "invq", "inq"):
            add_in(name if name != "inq" else "inq_was", a[name], whole(a[name]))
        for name in ("q", "k", "v", "g"):
            add_in(name, a[name], columns(step))
        add_in("q_gain", a["q_gain"], columns(step, 1))
        add_in("k_gain", a["k_gain"], columns(step, 1))
        if more:
            add_in("k_next", a["k"], columns(step + LAG))
            add_in("v_next", a["v"], columns(step + LAG))
        add_out("attn_out", (rows, width), bf16, columns(step), a.get("attn_out"))
        add_out("uq", (rows, width), f32, columns(step), a.get("uq"))
        add_out("gq", (1, width), f32, columns(step, 1), a.get("gq"))
        add_out("inq", (rows, HD), f32, whole(a["inq"]))
        add_out("dkv", pair_shape, f32, pair)
        add_out("send_r", pair_shape, bf16, pair)
        add_out("send_l", pair_shape, bf16, pair)
    if fin:
        group = step - LAG
        add_in("ink_was", a["ink"], whole(a["ink"]))
        add_in("k_fin", a["k"], columns(group))
        add_in("k_gain_fin", a["k_gain"], columns(group, 1))
        add_in("dkv_was", a["dkv"][group], pair)
        add_out("v_grad", (rows, width), bf16, columns(group), a.get("v_grad"))
        add_out("uk", (rows, width), f32, columns(group), a.get("uk"))
        add_out("gk", (1, width), f32, columns(group, 1), a.get("gk"))
        add_out("ink", (rows, HD), f32, whole(a["ink"]))
    scratch = []
    if attn:
        scratch = [
            pltpu.VMEM((3 * rows, HD), bf16),
            pltpu.VMEM((3 * rows, HD), bf16),
            pltpu.VMEM((HD, 3 * rows), bf16),
            pltpu.VMEM((HD, 3 * rows), bf16),
            pltpu.VMEM((rows, HD), bf16),
            pltpu.VMEM((3 * rows, HD), f32),
            pltpu.VMEM((3 * rows, HD), f32),
            pltpu.VMEM((rows, HD), f32),
        ]
    results = pl.pallas_call(
        functools.partial(
            step_kernel, rows, attn, fin, more,
            [i[0] for i in ins], [o[0] for o in outs],
        ),
        name=f"step_{step}",
        grid=(per,),
        in_specs=[i[2] for i in ins],
        out_specs=[o[2] for o in outs],
        out_shape=[o[1] for o in outs],
        input_output_aliases=aliases,
        scratch_shapes=scratch,
        cost_estimate=pl.CostEstimate(
            flops=per * (5 * 2 * rows * 3 * rows * HD if attn else rows * HD),
            transcendentals=per * rows * 3 * rows if attn else 0,
            bytes_accessed=per * rows * HD * 64,
        ),
    )(*[i[1] for i in ins])
    for (name, _, _), value in zip(outs, results):
        if name == "dkv":
            a["dkv"][step] = value
        elif name in ("send_r", "send_l"):
            a[name][step + LAG] = value
        else:
            a[name] = value


def body(q_raw, k_raw, values, out_grad, q_gain, k_gain, clip_lengths, clip_grid):
    rows, width = q_raw.shape
    heads = width // HD
    per = 2 if heads % 2 == 0 else 1
    groups = heads // per
    full_width = width * lax.axis_size("head")
    f32 = jnp.float32

    def raw_pair(group):
        at = slice(group * per * HD, (group + 1) * per * HD)
        return jnp.stack([k_raw[:, at], values[:, at]])

    a = {"send_r": {}, "send_l": {}, "recv_l": {}, "recv_r": {}, "dkv": {}}
    for step in range(min(LAG, groups)):
        a["send_r"][step] = a["send_l"][step] = raw_pair(step)

    def exchange(step):
        a["recv_l"][step] = passed_along(a["send_r"][step], "seq", 1)
        a["recv_r"][step] = passed_along(a["send_l"][step], "seq", -1)

    exchange(0)
    q_full, k_full = q_raw.astype(f32), k_raw.astype(f32)
    squares = lax.psum(
        jnp.stack([jnp.sum(q_full * q_full, axis=1), jnp.sum(k_full * k_full, axis=1)]), "head"
    )
    inverse = lax.rsqrt(squares / full_width + 1e-06)
    q_inv, k_inv = inverse[0][:, None], inverse[1][:, None]
    k_inv_window = jnp.concatenate(
        [passed_along(inverse[1], "seq", 1), inverse[1], passed_along(inverse[1], "seq", -1)]
    )
    first_pos = lax.axis_index("seq") * rows
    positions = first_pos - rows + jnp.arange(3 * rows, dtype=jnp.int32)
    labels, cosine, sine = window_tables(clip_lengths, clip_grid, positions)
    a.update(
        cos=cosine,
        sin=sine,
        invk=jnp.broadcast_to(k_inv_window[:, None], (3 * rows, HD)),
        invq=jnp.broadcast_to(q_inv, (rows, HD)),
        labk=jnp.broadcast_to(labels[:, None], (3 * rows, HD)),
        labq=jnp.repeat(labels[rows : 2 * rows].reshape(rows // TILE, TILE), 8, axis=0),
        inq=jnp.zeros((rows, HD), f32),
        ink=jnp.zeros((rows, HD), f32),
        q=q_raw, k=k_raw, v=values, g=out_grad,
        q_gain=q_gain[None, :], k_gain=k_gain[None, :],
    )
    for step in range(groups + LAG):
        if step + 1 < groups + LAG:
            exchange(step + 1) if step + 1 in a["send_r"] else None
        run_step(step, groups, per, rows, width, a)
        if step + 1 < groups + LAG and step + 1 not in a["recv_l"]:
            exchange(step + 1)

    def finished(unit_grad, raw, inv, inner_lanes):
        inner = lax.psum(jnp.sum(inner_lanes, axis=1), "head") / full_width
        unit = raw.astype(f32) * inv
        return (inv * (unit_grad - unit * inner[:, None])).astype(jnp.bfloat16)

    q_grad = finished(a["uq"], q_raw, q_inv, a["inq"])
    q_gain_grad = sum_over(a["gq"][0], "seq")
    k_gain_grad = sum_over(a["gk"][0], "seq")
    k_grad = finished(a["uk"], k_raw, k_inv, a["ink"])
    return (a["attn_out"], q_grad, k_grad, a["v_grad"], q_gain_grad, k_gain_grad)


def solution(mesh):
    rows = P(("dp", "seq"), "head")
    return jax.shard_map(
        body,
        mesh=mesh,
        in_specs=(rows, rows, rows, rows, P("head"), P("head"), P("dp"), P("dp", None)),
        out_specs=(rows, rows, rows, rows, P(("dp", "head")), P(("dp", "head"))),
        check_vma=False,
    )
```

```python
import functools
import math

import jax
import jax.numpy as jnp
from jax import lax
from jax.experimental import pallas as pl
from jax.experimental.pallas import tpu as pltpu
from jax.sharding import PartitionSpec as P

HD = 128
TILE = 128
LAG = 2
NEG = -1e30
SCALE = 1.0 / math.sqrt(HD)
EXP2_SCALE = SCALE * math.log2(math.e)
SPANS = (HD // 2 - 2 * (HD // 6), HD // 6, HD // 6)


def swapped_pairs(value, axis, start):
    pairs = []
    for i in range(start, lax.axis_size(axis) - 1, 2):
        pairs += [(i, i + 1), (i + 1, i)]
    return lax.ppermute(value, axis, pairs)


def sum_over(value, axis):
    count = lax.axis_size(axis)
    if count & (count - 1):
        return lax.psum(value, axis)
    step = 1
    while step < count:
        value = value + lax.ppermute(value, axis, [(i, i ^ step) for i in range(count)])
        step *= 2
    return value


def lane_freqs():
    tables = []
    for span_len in SPANS:
        exponent = jnp.arange(0, 2 * span_len, 2, dtype=jnp.float32) / (2 * span_len)
        tables.append(jnp.repeat(1.0 / 10000.0**exponent, 2))
    return jnp.concatenate(tables)


def upright(row):
    return jnp.broadcast_to(row, (TILE, TILE)).T


def laid(block):
    return jnp.sum(block.T, axis=0, keepdims=True)


def pair_swap(x):
    lane = lax.broadcasted_iota(jnp.int32, x.shape, 1)
    return jnp.where((lane & 1) == 0, pltpu.roll(x, HD - 1, 1), pltpu.roll(x, 1, 1))


def tables_kernel(rows, clips, first_ref, q, k, info, freqs, cos, sin, labk, labq, squares):
    f32 = jnp.float32
    for part, ref in ((0, q), (1, k)):
        total = jnp.zeros((TILE, HD), f32)
        for c in range(ref.shape[1] // HD):
            x = ref[:, c * HD : (c + 1) * HD].astype(f32)
            total += x * x
        squares[part * 8 : part * 8 + 8, :] = jnp.broadcast_to(laid(total), (8, HD))
    starts, ends = info[0:clips, :], info[clips : 2 * clips, :]
    number = lax.broadcasted_iota(jnp.int32, (clips, HD), 0).astype(f32) + 1.0
    lane = lax.broadcasted_iota(jnp.int32, (1, HD), 1)
    tile_at = first_ref[0] + pl.program_id(0) * TILE
    for seg in range(3):
        place = (tile_at + (seg - 1) * rows + lane).astype(f32)
        member = (place >= starts) & (place < ends)

        def pick(values):
            return jnp.sum(jnp.where(member, values, 0.0), axis=0, keepdims=True)

        label = pick(number) - 1.0
        labk[seg] = upright(label).astype(jnp.int32)
        if seg == 1:
            labq[...] = jnp.broadcast_to(label, (8, HD)).astype(jnp.int32)
            offset = place - pick(starts)
            height = jnp.maximum(pick(info[2 * clips : 3 * clips, :]), 1.0)
            across = jnp.maximum(pick(info[3 * clips : 4 * clips, :]), 1.0)
            frame = jnp.floor((offset + 0.5) / (height * across))
            rest = offset - frame * (height * across)
            row = jnp.floor((rest + 0.5) / across)
            col = rest - row * across
            wide = lax.broadcasted_iota(jnp.int32, (TILE, HD), 1)
            turn = jnp.where(
                wide < 2 * SPANS[0],
                upright(frame),
                jnp.where(wide < 2 * (SPANS[0] + SPANS[1]), upright(row), upright(col)),
            )
            angle = turn * freqs[0:1, :]
            cos[...] = jnp.cos(angle)
            sin[...] = jnp.where((wide & 1) == 0, -1.0, 1.0) * jnp.sin(angle)


def heads_kernel(rows, full_width, squares, cos, sin, k, v, gain, invq, invk, krot, send):
    f32 = jnp.float32

    @pl.when(pl.program_id(0) == 0)
    def _():
        for i in range(rows // TILE):
            at = slice(i * TILE, (i + 1) * TILE)
            for part, out in ((0, invq), (1, invk)):
                row = squares[i * 16 + part * 8 : i * 16 + part * 8 + 1, :]
                out[at, :] = upright(lax.rsqrt(row / full_width + 1e-06))

    x = k[...].astype(f32) * invk[...] * gain[1:2, :]
    turned = (x * cos[...] + pair_swap(x) * sin[...]).astype(jnp.bfloat16)
    krot[...] = turned
    send[0] = turned
    send[1] = v[...]


def step_kernel(rows, attn, fin, more, names_in, names_out, *refs):
    r = dict(zip(names_in + names_out, refs))
    f32, bf16 = jnp.float32, jnp.bfloat16
    first = pl.program_id(0) == 0
    own = slice(rows, 2 * rows)
    labk, cos, sin, invk = r["labk"], r["cos"], r["sin"], r["invk"]
    shared = []
    for side in (0, 1):
        edge = jnp.where(
            r["halo_at"][side] == 0, labk[rows - 1 : rows, :], labk[2 * rows : 2 * rows + 1, :]
        )
        shared.append(labk[own, :] == edge)

    def turned_back(x):
        return x * cos[...] - pair_swap(x) * sin[...]

    def dot(a, b, ca, cb):
        return lax.dot_general(a, b, (((ca,), (cb,)), ((), ())), preferred_element_type=f32)

    if attn:
        ksc, vsc, ktsc, vtsc, qsc, dksc, dvsc, dqsc = refs[len(names_in) + len(names_out) :]
        halo = [pl.ds(pl.multiple_of(r["halo_at"][side], TILE), rows) for side in (0, 1)]
        sources = (
            (r["recv_0"][0], r["recv_0"][1], halo[0]),
            (r["krot"][...], r["v"][...], own),
            (r["recv_1"][0], r["recv_1"][1], halo[1]),
        )
        for k_src, v_src, at in sources:
            ksc[at, :] = k_src
            vsc[at, :] = v_src
            ktsc[:, at] = k_src.T
            vtsc[:, at] = v_src.T
        q_unit = r["q"][...].astype(f32) * r["invq"][...]
        x = q_unit * r["gain"][0:1, :]
        qsc[...] = (x * cos[...] + pair_swap(x) * sin[...]).astype(bf16)
        dksc[...] = jnp.zeros_like(dksc)
        dvsc[...] = jnp.zeros_like(dvsc)
        tiles = rows // TILE
        reach = (2 * tiles + 1) * TILE

        def weigh(i):
            qs, ks = slice(i * TILE, (i + 1) * TILE), slice(i * TILE, i * TILE + reach)
            s = dot(ksc[ks, :], qsc[qs, :], 1, 1)
            allowed = labk[ks, :] == r["labq"][i * 8 : i * 8 + 1, :]
            s = jnp.where(allowed, s, NEG)
            top = jnp.max(s, axis=0, keepdims=True)
            p = jnp.exp2((s - top) * EXP2_SCALE)
            return p * (1.0 / jnp.sum(p, axis=0, keepdims=True))

        def attend(i, w):
            qs, ks = slice(i * TILE, (i + 1) * TILE), slice(i * TILE, i * TILE + reach)
            q_tile, g_tile = qsc[qs, :], r["g"][qs, :]
            wb = w.astype(bf16)
            out_t = dot(vtsc[:, ks], wb, 1, 0).astype(bf16)
            delta = jnp.sum(out_t.astype(f32) * g_tile.T.astype(f32), axis=0, keepdims=True)
            r["attn_out"][qs, :] = out_t.T
            dp = dot(vsc[ks, :], g_tile, 1, 1)
            ds = (w * (dp - delta)).astype(bf16)
            dqsc[qs, :] = dot(ktsc[:, ks], ds, 1, 0).T * SCALE
            dksc[ks, :] += dot(ds, q_tile, 1, 0)
            dvsc[ks, :] += dot(wb, g_tile, 1, 0)

        w = weigh(0)
        for i in range(tiles):
            w_next = weigh(i + 1) if i + 1 < tiles else None
            attend(i, w)
            w = w_next

        ahead = [None, None]
        if more:
            x = r["k_next"][...].astype(f32) * invk[...] * r["gain_next"][1:2, :]
            x = (x * cos[...] + pair_swap(x) * sin[...]).astype(bf16)
            r["krot_next"][...] = x
            ahead = [x.astype(f32), r["v_next"][...].astype(f32)]
        for part, acc, scale in ((0, dksc, SCALE), (1, dvsc, 1.0)):
            for side in (0, 1):
                back = acc[halo[side], :] * scale
                if more:
                    back = jnp.where(shared[side], ahead[part], back)
                r[f"send_{side}"][part] = back.astype(bf16)
            r["dkv"][part] = acc[own, :] * scale
        dq_pre = turned_back(dqsc[...])
        r["gq"][...] = jnp.sum(dq_pre * q_unit, axis=0, keepdims=True)
        uq = dq_pre * r["gain"][0:1, :]
        r["uq"][...] = uq

        @pl.when(first)
        def _():
            r["inq"][...] = r["inq_was"][...] if "inq_was" in r else jnp.zeros((rows, HD), f32)

        r["inq"][...] += uq * q_unit

    if fin:
        totals = []
        for part in (0, 1):
            total = r["dkv_was"][part]
            for side in (0, 1):
                total += jnp.where(shared[side], r[f"recv_{side}"][part].astype(f32), 0.0)
            totals.append(total)
        r["v_grad"][...] = totals[1].astype(bf16)
        k_unit = r["k_fin"][...].astype(f32) * invk[...]
        dk_pre = turned_back(totals[0])
        r["gk"][...] = jnp.sum(dk_pre * k_unit, axis=0, keepdims=True)
        uk = dk_pre * r["gain_fin"][1:2, :]
        r["uk"][...] = uk

        @pl.when(first)
        def _():
            r["ink"][...] = r["ink_was"][...] if "ink_was" in r else jnp.zeros((rows, HD), f32)

        r["ink"][...] += uk * k_unit


def whole(array):
    return pl.BlockSpec(array.shape, lambda j: (0,) * array.ndim)


def run_step(step, groups, per, rows, width, a):
    attn, fin, more = step < groups, step >= LAG, step + LAG < groups
    f32, bf16 = jnp.float32, jnp.bfloat16
    ins, outs, aliases = [], [], {}

    def columns(group, height=rows):
        return pl.BlockSpec((height, HD), lambda j: (0, group * per + j))

    local = pl.BlockSpec((rows, HD), lambda j: (0, j))
    pair = pl.BlockSpec((2, rows, HD), lambda j: (0, 0, j))
    pair_shape = (2, rows, per * HD)

    def add_in(name, array, spec=None):
        ins.append((name, array, whole(array) if spec is None else spec))

    def add_out(name, shape, dtype, spec, was=None):
        if was is not None:
            aliases[len(ins)] = len(outs)
            add_in(name + "_buf", was, pl.BlockSpec(memory_space=pl.ANY))
        outs.append((name, jax.ShapeDtypeStruct(shape, dtype), spec))

    for name in ("cos", "sin", "invk", "labk"):
        add_in(name, a[name])
    add_in("halo_at", a["halo_at"], pl.BlockSpec(memory_space=pltpu.SMEM))
    for side in (0, 1):
        add_in(f"recv_{side}", a["recv"][step][side], pair)
    sums = pl.BlockSpec((rows, HD), lambda j: (0, 0))
    if attn:
        for name in ("labq", "invq"):
            add_in(name, a[name])
        if "inq" in a:
            add_in("inq_was", a["inq"])
        for name in ("q", "v", "g"):
            add_in(name, a[name], columns(step))
        krot_at = 0 if step >= LAG else step * per
        add_in(
            "krot",
            a["krot"][step],
            pl.BlockSpec((rows, HD), lambda j: (0, krot_at + j)),
        )
        add_in("gain", a["gain"], columns(step, 2))
        if more:
            add_in("k_next", a["k"], columns(step + LAG))
            add_in("v_next", a["v"], columns(step + LAG))
            add_in("gain_next", a["gain"], columns(step + LAG, 2))
            add_out("krot_next", (rows, per * HD), bf16, local)
        add_out("attn_out", (rows, width), bf16, columns(step), a.get("attn_out"))
        add_out("uq", (rows, width), f32, columns(step), a.get("uq"))
        add_out("gq", (1, width), f32, columns(step, 1), a.get("gq"))
        add_out("inq", (rows, HD), f32, sums)
        add_out("dkv", pair_shape, f32, pair)
        add_out("send_0", pair_shape, bf16, pair)
        add_out("send_1", pair_shape, bf16, pair)
    if fin:
        group = step - LAG
        if "ink" in a:
            add_in("ink_was", a["ink"])
        add_in("k_fin", a["k"], columns(group))
        add_in("gain_fin", a["gain"], columns(group, 2))
        add_in("dkv_was", a["dkv"][group], pair)
        add_out("v_grad", (rows, width), bf16, columns(group), a.get("v_grad"))
        add_out("uk", (rows, width), f32, columns(group), a.get("uk"))
        add_out("gk", (1, width), f32, columns(group, 1), a.get("gk"))
        add_out("ink", (rows, HD), f32, sums)
    scratch = []
    if attn:
        scratch = [
            pltpu.VMEM((3 * rows, HD), bf16),
            pltpu.VMEM((3 * rows, HD), bf16),
            pltpu.VMEM((HD, 3 * rows), bf16),
            pltpu.VMEM((HD, 3 * rows), bf16),
            pltpu.VMEM((rows, HD), bf16),
            pltpu.VMEM((3 * rows, HD), f32),
            pltpu.VMEM((3 * rows, HD), f32),
            pltpu.VMEM((rows, HD), f32),
        ]
    results = pl.pallas_call(
        functools.partial(
            step_kernel, rows, attn, fin, more,
            [i[0] for i in ins], [o[0] for o in outs],
        ),
        grid=(per,),
        in_specs=[i[2] for i in ins],
        out_specs=[o[2] for o in outs],
        out_shape=[o[1] for o in outs],
        input_output_aliases=aliases,
        scratch_shapes=scratch,
        cost_estimate=pl.CostEstimate(
            flops=per * (5 * 2 * rows * 3 * rows * HD if attn else rows * HD),
            transcendentals=per * rows * 3 * rows if attn else 0,
            bytes_accessed=per * rows * HD * 64,
        ),
    )(*[i[1] for i in ins])
    for (name, _, _), value in zip(outs, results):
        if name == "dkv":
            a["dkv"][step] = value
        elif name == "krot_next":
            a["krot"][step + LAG] = value
        elif name in ("send_0", "send_1"):
            a["send"].setdefault(step + LAG, []).append(value)
        else:
            a[name] = value


def body(q_raw, k_raw, values, out_grad, q_gain, k_gain, clip_lengths, clip_grid):
    rows, width = q_raw.shape
    heads = width // HD
    per = 2 if heads % 2 == 0 else 1
    groups = heads // per
    tiles = rows // TILE
    clips = clip_lengths.shape[0]
    full_width = width * lax.axis_size("head")
    f32, bf16, i32 = jnp.float32, jnp.bfloat16, jnp.int32

    ends = jnp.cumsum(clip_lengths)
    info = jnp.concatenate([ends - clip_lengths, ends, clip_grid[:, 0], clip_grid[:, 1]])
    info = jnp.broadcast_to(info.astype(f32)[:, None], (4 * clips, HD))
    place = lax.axis_index("seq")
    block = pl.BlockSpec((TILE, HD), lambda i: (i, 0))
    wide = pl.BlockSpec((TILE, width), lambda i: (i, 0))
    freqs = jnp.broadcast_to(lane_freqs()[None, :], (8, HD))
    cosine, sine, labk, labq, squares = pl.pallas_call(
        functools.partial(tables_kernel, rows, clips),
        name="tables",
        grid=(tiles,),
        in_specs=[pl.BlockSpec(memory_space=pltpu.SMEM), wide, wide, whole(info), whole(freqs)],
        out_specs=[
            block,
            block,
            pl.BlockSpec((3, TILE, HD), lambda i: (0, i, 0)),
            pl.BlockSpec((8, HD), lambda i: (i, 0)),
            pl.BlockSpec((16, HD), lambda i: (i, 0)),
        ],
        out_shape=[
            jax.ShapeDtypeStruct((rows, HD), f32),
            jax.ShapeDtypeStruct((rows, HD), f32),
            jax.ShapeDtypeStruct((3, rows, HD), i32),
            jax.ShapeDtypeStruct((8 * tiles, HD), i32),
            jax.ShapeDtypeStruct((16 * tiles, HD), f32),
        ],
    )((place * rows).astype(i32)[None], q_raw, k_raw, info, freqs)
    squares = lax.psum(squares, "head")
    gain = jnp.stack([q_gain, k_gain])
    ready = min(LAG, groups)
    column = pl.BlockSpec((rows, HD), lambda j: (0, j))
    invq, invk, krot, send = pl.pallas_call(
        functools.partial(heads_kernel, rows, full_width),
        name="heads",
        grid=(ready * per,),
        in_specs=[
            whole(squares), whole(cosine), whole(sine), column, column,
            pl.BlockSpec((2, HD), lambda j: (0, j)),
        ],
        out_specs=[
            whole(cosine), whole(cosine), column,
            pl.BlockSpec((None, 2, rows, HD), lambda j: (j // per, 0, 0, j % per)),
        ],
        out_shape=[
            jax.ShapeDtypeStruct((rows, HD), f32),
            jax.ShapeDtypeStruct((rows, HD), f32),
            jax.ShapeDtypeStruct((rows, ready * per * HD), bf16),
            jax.ShapeDtypeStruct((ready, 2, rows, per * HD), bf16),
        ],
    )(squares, cosine, sine, k_raw, values, gain)

    a = {"recv": {}, "dkv": {}, "krot": {}, "send": {}}
    left_first = jnp.array([0, 2 * rows], i32)
    a.update(
        cos=cosine, sin=sine, labq=labq, labk=labk.reshape(3 * rows, HD),
        halo_at=jnp.where(place % 2 == 1, left_first, left_first[::-1]),
        invq=invq, invk=invk, q=q_raw, k=k_raw, v=values, g=out_grad, gain=gain,
    )

    def exchange(step):
        a["recv"][step] = [
            swapped_pairs(a["send"][step][side], "seq", side) for side in (0, 1)
        ]

    for step in range(ready):
        a["krot"][step] = krot
        a["send"][step] = [send[step]] * 2
        exchange(step)

    def finished(unit_grad, raw, inv, inner_lanes):
        inner = lax.psum(jnp.sum(inner_lanes, axis=1), "head") / full_width
        inv = inv[:, 0:1]
        unit = raw.astype(f32) * inv
        return (inv * (unit_grad - unit * inner[:, None])).astype(jnp.bfloat16)

    for step in range(groups):
        run_step(step, groups, per, rows, width, a)
        exchange(step + LAG)
    q_grad = finished(a["uq"], q_raw, invq, a["inq"])
    for step in range(groups, groups + LAG):
        if step == groups + LAG - 1:
            a["ink"], q_grad = lax.optimization_barrier((a["ink"], q_grad))
        run_step(step, groups, per, rows, width, a)
    gains = sum_over(jnp.concatenate([a["gq"], a["gk"]], 1)[0], "seq")
    k_grad = finished(a["uk"], k_raw, invk, a["ink"])
    return (a["attn_out"], q_grad, k_grad, a["v_grad"], gains[:width], gains[width:])


def solution(mesh):
    rows = P(("dp", "seq"), "head")

    return jax.shard_map(
        body,
        mesh=mesh,
        in_specs=(rows, rows, rows, rows, P("head"), P("head"), P("dp"), P("dp", None)),
        out_specs=(rows, rows, rows, rows, P(("dp", "head")), P(("dp", "head"))),
        check_vma=False,
    )
```
